128 devices in a mesh: wave: 8 (over y, z_lo), pix: 16 (over x, z_hi, core).
Axes of the slice: x: 4, y: 4, z: 4 (z_hi: 2, z_lo: 2; z = z_hi * 2 + z_lo), core: 2. Of those that a mesh axis runs over, the one named last changes fastest.
Arguments:
- raw_spectra: bfloat16 [2, 2, 16384, 2048], P(None, None, 'wave', 'pix'), may hold values from -6 to 6
- background: float32 [16384], P('wave'), may hold values from -6 to 6
- dispersion: float32 [16384], P('wave'), may hold values from -3.140625 to 3.140625
- propagator: bfloat16 [2, 2048, 2048], P(None, None, 'pix'), may hold values from -0.09375 to 0.09375
Outputs:
- image: float32 [2, 2, 16384, 2048], P(None, None, ('wave', 'pix'))
The draws below stay inside these ranges and needn't reach their ends.
All inputs are finite; a program needn't handle non-finite values.
Results may differ from the reference program's by a relative error of at most 0.0029.
Values may be sent and summed in bfloat16 or wider, within the bound.
A program may use at most 128 MiB of HBM per device.

```python
import jax
import jax.numpy as jnp

K = 16384
PIX = 2048
ROWS = 2


def shard_levels(stream_key, extent, split, low, top_value):
    level, own = 1.0, jax.random.fold_in(stream_key, 6)
    for position, blocks in split:
        heights = jnp.exp(jax.random.uniform(jax.random.fold_in(own, position), (blocks,), jnp.float32, low / len(split), top_value / len(split)))
        level = level * jnp.repeat(heights, extent[position] // blocks).reshape([-1 if axis == position else 1 for axis in range(len(extent))])
    return level


def noise(key, dims, width, most, pieces=(), dtype=jnp.bfloat16):
    result = jax.random.normal(key, dims, jnp.float32) * width
    if len(pieces) > 0:
        result = shard_levels(key, dims, pieces, -0.22, 0.18) * result
    return jnp.clip(result, min=-most, max=most).astype(dtype)


def setup_inputs(seed: int = 0) -> dict:
    arg_keys = jax.random.split(jax.random.key(seed), 5)
    return {
        "raw_spectra": noise(arg_keys[0], (2, ROWS, K, PIX), 1.0, 6.0, ((2, 8), (3, 16))),
        "background": noise(arg_keys[1], (K,), 1.0, 6.0, ((0, 8),), jnp.float32),
        "dispersion": jnp.clip(jax.random.uniform(arg_keys[2], (K,), jnp.float32, -3.140625, 3.140625), -3.140625, 3.140625),
        "propagator": noise(arg_keys[3], (2, PIX, PIX), (2 * PIX) ** -0.5, 0.09375, ((2, 16),)),
    }


def reference(raw_spectra, background, dispersion, propagator):
    real_part = raw_spectra[0].astype(jnp.float32) - background[None, :, None]
    imag_part = raw_spectra[1].astype(jnp.float32)
    cosine = jnp.cos(dispersion)[None, :, None]
    sine_part = jnp.sin(dispersion)[None, :, None]
    turned = real_part * cosine - imag_part * sine_part + 1j * (real_part * sine_part + imag_part * cosine)
    transform = jnp.fft.fft(turned, axis=1) / jnp.sqrt(jnp.float32(K))
    depth_real = jnp.real(transform).astype(jnp.bfloat16)
    depth_imag = jnp.imag(transform).astype(jnp.bfloat16)
    prop_real = propagator[0]
    prop_imag = propagator[1]
    image_real = jnp.dot(depth_real, prop_real, preferred_element_type=jnp.float32) - jnp.dot(depth_imag, prop_imag, preferred_element_type=jnp.float32)
    image_imag = jnp.dot(depth_real, prop_imag, preferred_element_type=jnp.float32) + jnp.dot(depth_imag, prop_real, preferred_element_type=jnp.float32)
    return jnp.stack((image_real, image_imag))
```

```python
import math

import jax
import jax.numpy as jnp
from jax import lax
from jax.sharding import PartitionSpec as P

HIGHEST_PRECISION = lax.Precision.HIGHEST


def twiddle_table(left_index, right_index, modulus, scale=1.0):
    product = left_index[:, None] * right_index[None, :] % modulus
    phase_angle = -2.0 * math.pi / modulus * product.astype(jnp.float32)
    return (jnp.cos(phase_angle) * scale, jnp.sin(phase_angle) * scale)


def complex_contract(spec, real, imag, cosine, sine_part):
    def dot(a, b):
        return jnp.einsum(spec, a, b, precision=HIGHEST_PRECISION)

    return (dot(real, cosine) - dot(imag, sine_part), dot(real, sine_part) + dot(imag, cosine))


def on_device(raw_spectra, background, dispersion, propagator):
    row_count = raw_spectra.shape[1]
    wave_span = raw_spectra.shape[2]
    pix_local = raw_spectra.shape[3]
    wave_count = lax.axis_size("wave")
    pix_count = lax.axis_size("pix")
    devices = wave_count * pix_count
    length = wave_span * wave_count
    sub_pix = pix_local // wave_count
    first = length // devices
    second = devices

    pieces = raw_spectra.reshape(2, row_count, wave_span, wave_count, sub_pix)
    pieces = jnp.transpose(pieces, (3, 0, 1, 4, 2))
    pieces = lax.all_to_all(pieces, "wave", 0, 0, tiled=True)
    full_background = lax.all_gather(background, "wave", tiled=True)
    full_dispersion = lax.all_gather(dispersion, "wave", tiled=True)

    spectra = jnp.transpose(pieces, (1, 2, 3, 0, 4)).reshape(2, row_count, sub_pix, length)
    real_part = spectra[0].astype(jnp.float32) - full_background
    imag_part = spectra[1].astype(jnp.float32)
    cosine = jnp.cos(full_dispersion)
    sine_part = jnp.sin(full_dispersion)
    turned_real = real_part * cosine - imag_part * sine_part
    turned_imag = real_part * sine_part + imag_part * cosine

    shape = (row_count, sub_pix, first, second)
    turned_real = turned_real.reshape(shape)
    turned_imag = turned_imag.reshape(shape)
    index_first = jnp.arange(first, dtype=jnp.int32)
    index_second = jnp.arange(second, dtype=jnp.int32)
    small_cos, small_sin = twiddle_table(index_first, index_first, first)
    stage_real, stage_imag = complex_contract(
        "rsak,az->rszk", turned_real, turned_imag, small_cos, small_sin
    )
    turn_cos, turn_sin = twiddle_table(index_first, index_second, length)
    mixed_real = stage_real * turn_cos - stage_imag * turn_sin
    mixed_imag = stage_real * turn_sin + stage_imag * turn_cos
    big_cos, big_sin = twiddle_table(
        index_second, index_second, second, 1.0 / math.sqrt(length)
    )
    out_real, out_imag = complex_contract(
        "rszk,kt->trsz", mixed_real, mixed_imag, big_cos, big_sin
    )
    depth_bf = jnp.stack((out_real, out_imag), axis=1).astype(jnp.bfloat16)
    arrived = lax.all_to_all(depth_bf, ("wave", "pix"), 0, 0, tiled=True)
    arrived = arrived.reshape(wave_count, pix_count, 2, row_count, sub_pix, first)
    depth_field = jnp.transpose(arrived, (2, 3, 5, 1, 0, 4)).reshape(
        2, row_count, first, pix_count * pix_local
    )
    column_piece = lax.all_gather(propagator, "pix", axis=2, tiled=True)
    image_real = jnp.dot(
        depth_field[0], column_piece[0], preferred_element_type=jnp.float32
    ) - jnp.dot(depth_field[1], column_piece[1], preferred_element_type=jnp.float32)
    image_imag = jnp.dot(
        depth_field[0], column_piece[1], preferred_element_type=jnp.float32
    ) + jnp.dot(depth_field[1], column_piece[0], preferred_element_type=jnp.float32)
    return jnp.stack((image_real, image_imag))


def solution(mesh):
    in_specs = (P(None, None, "wave", "pix"), P("wave"), P("wave"), P(None, None, "pix"))
    out_specs = P(None, None, ("wave", "pix"), None)
    return jax.shard_map(
        on_device, mesh=mesh, in_specs=in_specs, out_specs=out_specs, check_vma=False
    )
```

```python
import math

import jax
import jax.numpy as jnp
from jax import lax
from jax.sharding import PartitionSpec as P

HIGHEST_PRECISION = lax.Precision.HIGHEST


def twiddle_table(left_index, right_index, modulus, scale=1.0):
    product = left_index[:, None] * right_index[None, :] % modulus
    phase_angle = -2.0 * math.pi / modulus * product.astype(jnp.float32)
    return (jnp.cos(phase_angle) * scale, jnp.sin(phase_angle) * scale)


def complex_contract(spec, real, imag, cosine, sine_part):
    def dot(a, b):
        return jnp.einsum(spec, a, b, precision=HIGHEST_PRECISION)

    return (dot(real, cosine) - dot(imag, sine_part), dot(real, sine_part) + dot(imag, cosine))


def on_device(raw_spectra, background, dispersion, propagator):
    row_count = raw_spectra.shape[1]
    wave_span = raw_spectra.shape[2]
    pix_local = raw_spectra.shape[3]
    wave_count = lax.axis_size("wave")
    pix_count = lax.axis_size("pix")
    devices = wave_count * pix_count
    length = wave_span * wave_count
    sub_pix = pix_local // wave_count
    first = length // devices
    second = devices

    pieces = raw_spectra.reshape(2, row_count, wave_span, wave_count, sub_pix)
    pieces = jnp.transpose(pieces, (3, 0, 1, 4, 2))
    pieces = lax.all_to_all(pieces, "wave", 0, 0, tiled=True)
    tables = jnp.broadcast_to(
        jnp.stack((background, dispersion))[None], (wave_count, 2, wave_span)
    )
    tables = lax.all_to_all(tables, "wave", 0, 0, tiled=True)
    full_background = tables[:, 0].reshape(length)
    full_dispersion = tables[:, 1].reshape(length)

    spectra = jnp.transpose(pieces, (1, 2, 3, 0, 4)).reshape(2, row_count, sub_pix, length)
    real_part = spectra[0].astype(jnp.float32) - full_background
    imag_part = spectra[1].astype(jnp.float32)
    cosine = jnp.cos(full_dispersion)
    sine_part = jnp.sin(full_dispersion)
    turned_real = real_part * cosine - imag_part * sine_part
    turned_imag = real_part * sine_part + imag_part * cosine

    shape = (row_count, sub_pix, first, second)
    turned_real = turned_real.reshape(shape)
    turned_imag = turned_imag.reshape(shape)
    index_first = jnp.arange(first, dtype=jnp.int32)
    index_second = jnp.arange(second, dtype=jnp.int32)
    small_cos, small_sin = twiddle_table(index_first, index_first, first)
    stage_real, stage_imag = complex_contract(
        "rsak,az->rszk", turned_real, turned_imag, small_cos, small_sin
    )
    turn_cos, turn_sin = twiddle_table(index_first, index_second, length)
    mixed_real = stage_real * turn_cos - stage_imag * turn_sin
    mixed_imag = stage_real * turn_sin + stage_imag * turn_cos
    big_cos, big_sin = twiddle_table(
        index_second, index_second, second, 1.0 / math.sqrt(length)
    )
    out_real, out_imag = complex_contract(
        "rszk,kt->trsz", mixed_real, mixed_imag, big_cos, big_sin
    )
    depth_bf = jnp.stack((out_real, out_imag), axis=1).astype(jnp.bfloat16)
    arrived = lax.all_to_all(depth_bf, ("wave", "pix"), 0, 0, tiled=True)
    arrived = arrived.reshape(wave_count, pix_count, 2, row_count, sub_pix, first)
    depth_field = jnp.transpose(arrived, (2, 3, 5, 1, 0, 4)).reshape(
        2, row_count, first, pix_count * pix_local
    )
    column_piece = lax.all_gather(propagator, "pix", axis=2, tiled=True)
    image_real = jnp.dot(
        depth_field[0], column_piece[0], preferred_element_type=jnp.float32
    ) - jnp.dot(depth_field[1], column_piece[1], preferred_element_type=jnp.float32)
    image_imag = jnp.dot(
        depth_field[0], column_piece[1], preferred_element_type=jnp.float32
    ) + jnp.dot(depth_field[1], column_piece[0], preferred_element_type=jnp.float32)
    return jnp.stack((image_real, image_imag))


def solution(mesh):
    in_specs = (P(None, None, "wave", "pix"), P("wave"), P("wave"), P(None, None, "pix"))
    out_specs = P(None, None, ("wave", "pix"), None)
    return jax.shard_map(
        on_device, mesh=mesh, in_specs=in_specs, out_specs=out_specs, check_vma=False
    )
```

```python
import math

import jax
import jax.numpy as jnp
from jax import lax
from jax.sharding import PartitionSpec as P

HIGHEST_PRECISION = lax.Precision.HIGHEST


def twiddle_table(left_index, right_index, modulus, scale=1.0):
    product = left_index[:, None] * right_index[None, :] % modulus
    phase_angle = -2.0 * math.pi / modulus * product.astype(jnp.float32)
    return (jnp.cos(phase_angle) * scale, jnp.sin(phase_angle) * scale)


def complex_contract(spec, real, imag, cosine, sine_part):
    def dot(a, b):
        return jnp.einsum(spec, a, b, precision=HIGHEST_PRECISION)

    return (dot(real, cosine) - dot(imag, sine_part), dot(real, sine_part) + dot(imag, cosine))


def on_device(raw_spectra, background, dispersion, propagator):
    row_count = raw_spectra.shape[1]
    wave_span = raw_spectra.shape[2]
    pix_local = raw_spectra.shape[3]
    wave_count = lax.axis_size("wave")
    pix_count = lax.axis_size("pix")
    devices = wave_count * pix_count
    length = wave_span * wave_count
    sub_pix = pix_local // wave_count
    first = length // devices
    second = devices

    pieces = raw_spectra.reshape(2, row_count, wave_span, wave_count, sub_pix)
    pieces = jnp.transpose(pieces, (3, 0, 1, 4, 2))
    pieces = lax.all_to_all(pieces, "wave", 0, 0, tiled=True)
    tables = jnp.broadcast_to(
        jnp.stack((background, dispersion))[None], (wave_count, 2, wave_span)
    )
    tables = lax.all_to_all(tables, "wave", 0, 0, tiled=True)
    full_background = tables[:, 0].reshape(length)
    full_dispersion = tables[:, 1].reshape(length)

    spectra = jnp.transpose(pieces, (1, 2, 3, 0, 4)).reshape(2, row_count, sub_pix, length)
    real_part = spectra[0].astype(jnp.float32) - full_background
    imag_part = spectra[1].astype(jnp.float32)
    cosine = jnp.cos(full_dispersion)
    sine_part = jnp.sin(full_dispersion)
    turned_real = real_part * cosine - imag_part * sine_part
    turned_imag = real_part * sine_part + imag_part * cosine

    shape = (row_count, sub_pix, first, second)
    turned_real = turned_real.reshape(shape)
    turned_imag = turned_imag.reshape(shape)
    index_first = jnp.arange(first, dtype=jnp.int32)
    index_second = jnp.arange(second, dtype=jnp.int32)
    small_cos, small_sin = twiddle_table(index_first, index_first, first)
    stage_real, stage_imag = complex_contract(
        "rsak,az->rszk", turned_real, turned_imag, small_cos, small_sin
    )
    turn_cos, turn_sin = twiddle_table(index_first, index_second, length)
    mixed_real = stage_real * turn_cos - stage_imag * turn_sin
    mixed_imag = stage_real * turn_sin + stage_imag * turn_cos
    big_cos, big_sin = twiddle_table(
        index_second, index_second, second, 1.0 / math.sqrt(length)
    )
    out_real, out_imag = complex_contract(
        "rszk,kt->trsz", mixed_real, mixed_imag, big_cos, big_sin
    )
    depth_bf = jnp.stack((out_real, out_imag), axis=1).astype(jnp.bfloat16)
    arrived = lax.all_to_all(depth_bf, ("wave", "pix"), 0, 0, tiled=True)
    arrived = arrived.reshape(wave_count, pix_count, 2, row_count, sub_pix, first)
    depth_field = jnp.transpose(arrived, (2, 3, 5, 1, 0, 4)).reshape(
        2, row_count, first, pix_count * pix_local
    )
    held, sibling = gather_columns(propagator, wave_count, pix_count)
    columns = jnp.stack((held, sibling), axis=1)
    image_real = jnp.einsum(
        "rzp,ocpj->rzocj", depth_field[0], columns[:, :, 0], preferred_element_type=jnp.float32
    ) - jnp.einsum(
        "rzp,ocpj->rzocj", depth_field[1], columns[:, :, 1], preferred_element_type=jnp.float32
    )
    image_imag = jnp.einsum(
        "rzp,ocpj->rzocj", depth_field[0], columns[:, :, 1], preferred_element_type=jnp.float32
    ) + jnp.einsum(
        "rzp,ocpj->rzocj", depth_field[1], columns[:, :, 0], preferred_element_type=jnp.float32
    )
    image = jnp.stack((image_real, image_imag))
    chip_count = pix_count // 2
    pix_pos = lax.axis_index("pix")
    order = [(-offset) % chip_count for offset in range(chip_count)]
    image = image[:, :, :, jnp.array(order, dtype=jnp.int32)]
    image = jnp.roll(image, (pix_pos // 2, pix_pos % 2), axis=(3, 4))
    return image.reshape(2, row_count, first, pix_count * pix_local)


def gather_columns(propagator, wave_count, pix_count):
    chip_count = pix_count // 2

    def flat(wave, pix):
        return wave * pix_count + pix

    held = [propagator]
    for offset in range(1, chip_count):
        pairs = []
        for wave in range(wave_count):
            for pix in range(pix_count):
                target_chip = (pix // 2 + offset) % chip_count
                target_wave = wave if offset % 2 == 0 else wave ^ 1
                pairs.append((flat(wave, pix), flat(target_wave, 2 * target_chip + pix % 2)))
        held.append(lax.ppermute(propagator, ("wave", "pix"), pairs))
    held = jnp.stack(held)
    pairs = [
        (flat(wave, pix), flat(wave, pix ^ 1))
        for wave in range(wave_count)
        for pix in range(pix_count)
    ]
    sibling = lax.ppermute(held, ("wave", "pix"), pairs)
    return held, sibling


def solution(mesh):
    in_specs = (P(None, None, "wave", "pix"), P("wave"), P("wave"), P(None, None, "pix"))
    out_specs = P(None, None, ("wave", "pix"), None)
    return jax.shard_map(
        on_device, mesh=mesh, in_specs=in_specs, out_specs=out_specs, check_vma=False
    )
```

```python
import math

import jax
import jax.numpy as jnp
from jax import lax
from jax.sharding import PartitionSpec as P

HIGHEST_PRECISION = lax.Precision.HIGHEST
PIX = ("chip", "core")


def twiddle_table(left_index, right_index, modulus, scale=1.0):
    product = left_index[:, None] * right_index[None, :] % modulus
    phase_angle = -2.0 * math.pi / modulus * product.astype(jnp.float32)
    return (jnp.cos(phase_angle) * scale, jnp.sin(phase_angle) * scale)


def complex_contract(spec, real, imag, cosine, sine_part):
    def dot(a, b):
        return jnp.einsum(spec, a, b, precision=HIGHEST_PRECISION)

    return (dot(real, cosine) - dot(imag, sine_part), dot(real, sine_part) + dot(imag, cosine))


def on_device(raw_spectra, background, dispersion, propagator):
    row_count = raw_spectra.shape[1]
    wave_span = raw_spectra.shape[2]
    pix_local = raw_spectra.shape[3]
    wave_count = lax.axis_size("wave")
    pix_count = lax.axis_size(PIX)
    devices = wave_count * pix_count
    length = wave_span * wave_count
    sub_pix = pix_local // wave_count
    first = length // devices
    second = devices

    pieces = raw_spectra.reshape(2, row_count, wave_span, wave_count, sub_pix)
    pieces = jnp.transpose(pieces, (3, 0, 1, 4, 2))
    pieces = lax.all_to_all(pieces, "wave", 0, 0, tiled=True)
    tables = jnp.broadcast_to(
        jnp.stack((background, dispersion))[None], (wave_count, 2, wave_span)
    )
    tables = lax.all_to_all(tables, "wave", 0, 0, tiled=True)
    full_background = tables[:, 0].reshape(length)
    full_dispersion = tables[:, 1].reshape(length)

    spectra = jnp.transpose(pieces, (1, 2, 3, 0, 4)).reshape(2, row_count, sub_pix, length)
    real_part = spectra[0].astype(jnp.float32) - full_background
    imag_part = spectra[1].astype(jnp.float32)
    cosine = jnp.cos(full_dispersion)
    sine_part = jnp.sin(full_dispersion)
    turned_real = real_part * cosine - imag_part * sine_part
    turned_imag = real_part * sine_part + imag_part * cosine

    shape = (row_count, sub_pix, first, second)
    turned_real = turned_real.reshape(shape)
    turned_imag = turned_imag.reshape(shape)
    index_first = jnp.arange(first, dtype=jnp.int32)
    index_second = jnp.arange(second, dtype=jnp.int32)
    small_cos, small_sin = twiddle_table(index_first, index_first, first)
    stage_real, stage_imag = complex_contract(
        "rsak,az->rszk", turned_real, turned_imag, small_cos, small_sin
    )
    turn_cos, turn_sin = twiddle_table(index_first, index_second, length)
    mixed_real = stage_real * turn_cos - stage_imag * turn_sin
    mixed_imag = stage_real * turn_sin + stage_imag * turn_cos
    big_cos, big_sin = twiddle_table(
        index_second, index_second, second, 1.0 / math.sqrt(length)
    )
    out_real, out_imag = complex_contract(
        "rszk,kt->trsz", mixed_real, mixed_imag, big_cos, big_sin
    )
    depth_bf = jnp.stack((out_real, out_imag), axis=1).astype(jnp.bfloat16)
    same_core = lax.all_gather(propagator, "chip", axis=0)
    same_core, depth_bf = lax.optimization_barrier((same_core, depth_bf))
    arrived = lax.all_to_all(depth_bf, ("wave",) + PIX, 0, 0, tiled=True)
    arrived = arrived.reshape(wave_count, pix_count, 2, row_count, sub_pix, first)
    depth_field = jnp.transpose(arrived, (2, 3, 5, 1, 0, 4)).reshape(
        2, row_count, first, pix_count * pix_local
    )
    column_piece = lax.all_gather(same_core, "core", axis=0)
    image_real = jnp.einsum(
        "rzp,kcpj->rzckj", depth_field[0], column_piece[:, :, 0], preferred_element_type=jnp.float32
    ) - jnp.einsum(
        "rzp,kcpj->rzckj", depth_field[1], column_piece[:, :, 1], preferred_element_type=jnp.float32
    )
    image_imag = jnp.einsum(
        "rzp,kcpj->rzckj", depth_field[0], column_piece[:, :, 1], preferred_element_type=jnp.float32
    ) + jnp.einsum(
        "rzp,kcpj->rzckj", depth_field[1], column_piece[:, :, 0], preferred_element_type=jnp.float32
    )
    image = jnp.stack((image_real, image_imag))
    return image.reshape(2, row_count, first, pix_count * pix_local)


def solution(mesh):
    wave_count, pix_count = mesh.devices.shape
    split_mesh = jax.sharding.Mesh(
        mesh.devices.reshape(wave_count, pix_count // 2, 2), ("wave",) + PIX
    )
    in_specs = (P(None, None, "wave", PIX), P("wave"), P("wave"), P(None, None, PIX))
    out_specs = P(None, None, ("wave",) + PIX, None)
    return jax.shard_map(
        on_device, mesh=split_mesh, in_specs=in_specs, out_specs=out_specs, check_vma=False
    )
```

```python
import math

import jax
import jax.numpy as jnp
from jax import lax
from jax.sharding import PartitionSpec as P

HIGHEST_PRECISION = lax.Precision.HIGHEST
PIX = ("chip", "core")


def twiddle_table(left_index, right_index, modulus, scale=1.0):
    product = left_index[:, None] * right_index[None, :] % modulus
    phase_angle = -2.0 * math.pi / modulus * product.astype(jnp.float32)
    return (jnp.cos(phase_angle) * scale, jnp.sin(phase_angle) * scale)


def complex_contract(spec, real, imag, cosine, sine_part):
    def dot(a, b):
        return jnp.einsum(spec, a, b, precision=HIGHEST_PRECISION)

    return (dot(real, cosine) - dot(imag, sine_part), dot(real, sine_part) + dot(imag, cosine))


def on_device(raw_spectra, background, dispersion, propagator):
    row_count = raw_spectra.shape[1]
    wave_span = raw_spectra.shape[2]
    pix_local = raw_spectra.shape[3]
    wave_count = lax.axis_size("wave")
    pix_count = lax.axis_size(PIX)
    devices = wave_count * pix_count
    length = wave_span * wave_count
    sub_pix = pix_local // wave_count
    first = length // devices
    second = devices

    pieces = raw_spectra.reshape(2, row_count, wave_span, wave_count, sub_pix)
    pieces = jnp.transpose(pieces, (3, 0, 1, 4, 2))
    pieces = lax.all_to_all(pieces, "wave", 0, 0, tiled=True)
    tables = jnp.broadcast_to(
        jnp.stack((background, dispersion))[None], (wave_count, 2, wave_span)
    )
    tables = lax.all_to_all(tables, "wave", 0, 0, tiled=True)
    full_background = tables[:, 0].reshape(length)
    full_dispersion = tables[:, 1].reshape(length)

    spectra = jnp.transpose(pieces, (1, 2, 3, 0, 4)).reshape(2, row_count, sub_pix, length)
    real_part = spectra[0].astype(jnp.float32) - full_background
    imag_part = spectra[1].astype(jnp.float32)
    cosine = jnp.cos(full_dispersion)
    sine_part = jnp.sin(full_dispersion)
    turned_real = real_part * cosine - imag_part * sine_part
    turned_imag = real_part * sine_part + imag_part * cosine

    shape = (row_count, sub_pix, first, second)
    turned_real = turned_real.reshape(shape)
    turned_imag = turned_imag.reshape(shape)
    index_first = jnp.arange(first, dtype=jnp.int32)
    index_second = jnp.arange(second, dtype=jnp.int32)
    small_cos, small_sin = twiddle_table(index_first, index_first, first)
    stage_real, stage_imag = complex_contract(
        "rsak,az->rszk", turned_real, turned_imag, small_cos, small_sin
    )
    turn_cos, turn_sin = twiddle_table(index_first, index_second, length)
    mixed_real = stage_real * turn_cos - stage_imag * turn_sin
    mixed_imag = stage_real * turn_sin + stage_imag * turn_cos
    big_cos, big_sin = twiddle_table(
        index_second, index_second, second, 1.0 / math.sqrt(length)
    )
    out_real, out_imag = complex_contract(
        "rszk,kt->trsz", mixed_real, mixed_imag, big_cos, big_sin
    )
    depth_bf = jnp.stack((out_real, out_imag), axis=1).astype(jnp.bfloat16)
    slice_rows = propagator.shape[1] // wave_count
    own_rows = lax.dynamic_slice_in_dim(
        propagator, lax.axis_index("wave") * slice_rows, slice_rows, axis=1
    )
    same_core = lax.all_gather(own_rows, "chip", axis=0)
    same_core = lax.all_gather(same_core, "wave", axis=0)
    same_core, depth_bf = lax.optimization_barrier((same_core, depth_bf))
    arrived = lax.all_to_all(depth_bf, ("wave",) + PIX, 0, 0, tiled=True)
    arrived = arrived.reshape(wave_count, pix_count, 2, row_count, sub_pix, first)
    depth_field = jnp.transpose(arrived, (2, 3, 5, 1, 0, 4)).reshape(
        2, row_count, first, pix_count * pix_local
    )
    column_piece = lax.all_gather(same_core, "core", axis=0)
    depth_field = depth_field.reshape(2, row_count, first, wave_count, slice_rows)

    def product(depth, part):
        return jnp.einsum(
            "rzwi,kwcij->rzckj",
            depth,
            column_piece[:, :, :, part],
            preferred_element_type=jnp.float32,
        )

    image_real = product(depth_field[0], 0) - product(depth_field[1], 1)
    image_imag = product(depth_field[0], 1) + product(depth_field[1], 0)
    image = jnp.stack((image_real, image_imag))
    return image.reshape(2, row_count, first, pix_count * pix_local)


def solution(mesh):
    wave_count, pix_count = mesh.devices.shape
    split_mesh = jax.sharding.Mesh(
        mesh.devices.reshape(wave_count, pix_count // 2, 2), ("wave",) + PIX
    )
    in_specs = (P(None, None, "wave", PIX), P("wave"), P("wave"), P(None, None, PIX))
    out_specs = P(None, None, ("wave",) + PIX, None)
    return jax.shard_map(
        on_device, mesh=split_mesh, in_specs=in_specs, out_specs=out_specs, check_vma=False
    )
```

```python
import math

import jax
import jax.numpy as jnp
from jax import lax
from jax.sharding import PartitionSpec as P

HIGHEST_PRECISION = lax.Precision.HIGHEST


def twiddle_table(left_index, right_index, modulus, scale=1.0):
    product = left_index[:, None] * right_index[None, :] % modulus
    phase_angle = -2.0 * math.pi / modulus * product.astype(jnp.float32)
    return (jnp.cos(phase_angle) * scale, jnp.sin(phase_angle) * scale)


def complex_contract(spec, real, imag, cosine, sine_part):
    def dot(a, b):
        return jnp.einsum(spec, a, b, precision=HIGHEST_PRECISION)

    return (dot(real, cosine) - dot(imag, sine_part), dot(real, sine_part) + dot(imag, cosine))


def on_device(raw_spectra, background, dispersion, propagator):
    row_count = raw_spectra.shape[1]
    wave_span = raw_spectra.shape[2]
    pix_local = raw_spectra.shape[3]
    wave_count = lax.axis_size("wave")
    pix_count = lax.axis_size("pix")
    devices = wave_count * pix_count
    length = wave_span * wave_count
    sub_pix = pix_local // wave_count
    first = length // devices
    second = devices

    pieces = raw_spectra.reshape(2, row_count, wave_span, wave_count, sub_pix)
    pieces = jnp.transpose(pieces, (3, 0, 1, 4, 2))
    pieces = lax.all_to_all(pieces, "wave", 0, 0, tiled=True)
    tables = jnp.broadcast_to(
        jnp.stack((background, dispersion))[None], (wave_count, 2, wave_span)
    )
    tables = lax.all_to_all(tables, "wave", 0, 0, tiled=True)
    full_background = tables[:, 0].reshape(length)
    full_dispersion = tables[:, 1].reshape(length)

    spectra = jnp.transpose(pieces, (1, 2, 3, 0, 4)).reshape(2, row_count, sub_pix, length)
    real_part = spectra[0].astype(jnp.float32) - full_background
    imag_part = spectra[1].astype(jnp.float32)
    cosine = jnp.cos(full_dispersion)
    sine_part = jnp.sin(full_dispersion)
    turned_real = real_part * cosine - imag_part * sine_part
    turned_imag = real_part * sine_part + imag_part * cosine

    shape = (row_count, sub_pix, first, second)
    turned_real = turned_real.reshape(shape)
    turned_imag = turned_imag.reshape(shape)
    index_first = jnp.arange(first, dtype=jnp.int32)
    index_second = jnp.arange(second, dtype=jnp.int32)
    small_cos, small_sin = twiddle_table(index_first, index_first, first)
    stage_real, stage_imag = complex_contract(
        "rsak,az->rszk", turned_real, turned_imag, small_cos, small_sin
    )
    turn_cos, turn_sin = twiddle_table(index_first, index_second, length)
    mixed_real = stage_real * turn_cos - stage_imag * turn_sin
    mixed_imag = stage_real * turn_sin + stage_imag * turn_cos
    big_cos, big_sin = twiddle_table(
        index_second, index_second, second, 1.0 / math.sqrt(length)
    )
    out_real, out_imag = complex_contract(
        "rszk,kt->trsz", mixed_real, mixed_imag, big_cos, big_sin
    )
    depth_bf = jnp.stack((out_real, out_imag), axis=1).astype(jnp.bfloat16)
    held = gather_held(propagator, wave_count, pix_count)
    held, depth_bf = lax.optimization_barrier((held, depth_bf))
    arrived = lax.all_to_all(depth_bf, ("wave", "pix"), 0, 0, tiled=True)
    arrived = arrived.reshape(wave_count, pix_count, 2, row_count, sub_pix, first)
    depth_field = jnp.transpose(arrived, (2, 3, 5, 1, 0, 4)).reshape(
        2, row_count, first, pix_count * pix_local
    )
    sibling = swap_cores(held, wave_count, pix_count)
    columns = jnp.stack((held, sibling), axis=1)
    image_real = jnp.einsum(
        "rzp,ocpj->rzocj", depth_field[0], columns[:, :, 0], preferred_element_type=jnp.float32
    ) - jnp.einsum(
        "rzp,ocpj->rzocj", depth_field[1], columns[:, :, 1], preferred_element_type=jnp.float32
    )
    image_imag = jnp.einsum(
        "rzp,ocpj->rzocj", depth_field[0], columns[:, :, 1], preferred_element_type=jnp.float32
    ) + jnp.einsum(
        "rzp,ocpj->rzocj", depth_field[1], columns[:, :, 0], preferred_element_type=jnp.float32
    )
    image = jnp.stack((image_real, image_imag))
    chip_count = pix_count // 2
    pix_pos = lax.axis_index("pix")
    order = [(-offset) % chip_count for offset in range(chip_count)]
    image = image[:, :, :, jnp.array(order, dtype=jnp.int32)]
    image = jnp.roll(image, (pix_pos // 2, pix_pos % 2), axis=(3, 4))
    return image.reshape(2, row_count, first, pix_count * pix_local)


def flat_index(wave, pix, pix_count):
    return wave * pix_count + pix


def gather_held(propagator, wave_count, pix_count):
    chip_count = pix_count // 2
    held = [propagator]
    for offset in range(1, chip_count):
        pairs = []
        for wave in range(wave_count):
            for pix in range(pix_count):
                target_chip = (pix // 2 + offset) % chip_count
                target_wave = wave if offset % 2 == 0 else wave ^ 1
                pairs.append(
                    (
                        flat_index(wave, pix, pix_count),
                        flat_index(target_wave, 2 * target_chip + pix % 2, pix_count),
                    )
                )
        held.append(lax.ppermute(propagator, ("wave", "pix"), pairs))
    return jnp.stack(held)


def swap_cores(held, wave_count, pix_count):
    pairs = [
        (flat_index(wave, pix, pix_count), flat_index(wave, pix ^ 1, pix_count))
        for wave in range(wave_count)
        for pix in range(pix_count)
    ]
    return lax.ppermute(held, ("wave", "pix"), pairs)


def solution(mesh):
    in_specs = (P(None, None, "wave", "pix"), P("wave"), P("wave"), P(None, None, "pix"))
    out_specs = P(None, None, ("wave", "pix"), None)
    return jax.shard_map(
        on_device, mesh=mesh, in_specs=in_specs, out_specs=out_specs, check_vma=False
    )
```

```python
import math

import jax
import jax.numpy as jnp
from jax import lax
from jax.sharding import PartitionSpec as P

HIGHEST_PRECISION = lax.Precision.HIGHEST


def twiddle_table(left_index, right_index, modulus, scale=1.0):
    product = left_index[:, None] * right_index[None, :] % modulus
    phase_angle = -2.0 * math.pi / modulus * product.astype(jnp.float32)
    return (jnp.cos(phase_angle) * scale, jnp.sin(phase_angle) * scale)


def complex_contract(spec, real, imag, cosine, sine_part):
    def dot(a, b):
        return jnp.einsum(spec, a, b, precision=HIGHEST_PRECISION)

    return (dot(real, cosine) - dot(imag, sine_part), dot(real, sine_part) + dot(imag, cosine))


def on_device(raw_spectra, background, dispersion, propagator):
    row_count = raw_spectra.shape[1]
    wave_span = raw_spectra.shape[2]
    pix_local = raw_spectra.shape[3]
    wave_count = lax.axis_size("wave")
    pix_count = lax.axis_size("pix")
    devices = wave_count * pix_count
    length = wave_span * wave_count
    sub_pix = pix_local // wave_count
    first = length // devices
    second = devices

    pieces = raw_spectra.reshape(2, row_count, wave_span, wave_count, sub_pix)
    pieces = jnp.transpose(pieces, (3, 0, 1, 4, 2))
    pieces = lax.all_to_all(pieces, "wave", 0, 0, tiled=True)
    tables = jnp.broadcast_to(
        jnp.stack((background, dispersion))[None], (wave_count, 2, wave_span)
    )
    tables = lax.all_to_all(tables, "wave", 0, 0, tiled=True)
    full_background = tables[:, 0].reshape(length)
    full_dispersion = tables[:, 1].reshape(length)

    spectra = jnp.transpose(pieces, (1, 2, 3, 0, 4)).reshape(2, row_count, sub_pix, length)
    real_part = spectra[0].astype(jnp.float32) - full_background
    imag_part = spectra[1].astype(jnp.float32)
    cosine = jnp.cos(full_dispersion)
    sine_part = jnp.sin(full_dispersion)
    turned_real = real_part * cosine - imag_part * sine_part
    turned_imag = real_part * sine_part + imag_part * cosine

    shape = (row_count, sub_pix, first, second)
    turned_real = turned_real.reshape(shape)
    turned_imag = turned_imag.reshape(shape)
    index_first = jnp.arange(first, dtype=jnp.int32)
    index_second = jnp.arange(second, dtype=jnp.int32)
    small_cos, small_sin = twiddle_table(index_first, index_first, first)
    stage_real, stage_imag = complex_contract(
        "rsak,az->rszk", turned_real, turned_imag, small_cos, small_sin
    )
    turn_cos, turn_sin = twiddle_table(index_first, index_second, length)
    mixed_real = stage_real * turn_cos - stage_imag * turn_sin
    mixed_imag = stage_real * turn_sin + stage_imag * turn_cos
    big_cos, big_sin = twiddle_table(
        index_second, index_second, second, 1.0 / math.sqrt(length)
    )
    out_real, out_imag = complex_contract(
        "rszk,kt->trsz", mixed_real, mixed_imag, big_cos, big_sin
    )
    depth_bf = jnp.stack((out_real, out_imag), axis=1).astype(jnp.bfloat16)
    arrived = lax.all_to_all(depth_bf, ("wave", "pix"), 0, 0, tiled=True)
    arrived = arrived.reshape(wave_count, pix_count, 2, row_count, sub_pix, first)
    depth_field = jnp.transpose(arrived, (2, 3, 5, 1, 0, 4)).reshape(
        2, row_count, first, pix_count * pix_local
    )
    halves = 2
    half_rows = propagator.shape[1] // halves
    image_real = 0.0
    image_imag = 0.0
    for half in range(halves):
        rows = slice(half * half_rows, (half + 1) * half_rows)
        column_piece = lax.all_gather(propagator[:, rows], "pix", axis=2, tiled=True)
        depth_real = depth_field[0][:, :, rows]
        depth_imag = depth_field[1][:, :, rows]
        image_real = image_real + (
            jnp.dot(depth_real, column_piece[0], preferred_element_type=jnp.float32)
            - jnp.dot(depth_imag, column_piece[1], preferred_element_type=jnp.float32)
        )
        image_imag = image_imag + (
            jnp.dot(depth_real, column_piece[1], preferred_element_type=jnp.float32)
            + jnp.dot(depth_imag, column_piece[0], preferred_element_type=jnp.float32)
        )
    return jnp.stack((image_real, image_imag))


def solution(mesh):
    in_specs = (P(None, None, "wave", "pix"), P("wave"), P("wave"), P(None, None, "pix"))
    out_specs = P(None, None, ("wave", "pix"), None)
    return jax.shard_map(
        on_device, mesh=mesh, in_specs=in_specs, out_specs=out_specs, check_vma=False
    )
```

```python
import math

import jax
import jax.numpy as jnp
from jax import lax
from jax.sharding import PartitionSpec as P

HIGHEST_PRECISION = lax.Precision.HIGHEST


def twiddle_table(left_index, right_index, modulus, scale=1.0):
    product = left_index[:, None] * right_index[None, :] % modulus
    phase_angle = -2.0 * math.pi / modulus * product.astype(jnp.float32)
    return (jnp.cos(phase_angle) * scale, jnp.sin(phase_angle) * scale)


def complex_contract(spec, real, imag, cosine, sine_part):
    def dot(a, b):
        return jnp.einsum(spec, a, b, precision=HIGHEST_PRECISION)

    return (dot(real, cosine) - dot(imag, sine_part), dot(real, sine_part) + dot(imag, cosine))


def on_device(raw_spectra, background, dispersion, propagator):
    row_count = raw_spectra.shape[1]
    wave_span = raw_spectra.shape[2]
    pix_local = raw_spectra.shape[3]
    wave_count = lax.axis_size("wave")
    pix_count = lax.axis_size("pix")
    devices = wave_count * pix_count
    length = wave_span * wave_count
    sub_pix = pix_local // wave_count
    first = length // devices
    second = devices

    pieces = raw_spectra.reshape(2, row_count, wave_span, wave_count, sub_pix)
    pieces = jnp.transpose(pieces, (3, 0, 1, 4, 2))
    pieces = lax.all_to_all(pieces, "wave", 0, 0, tiled=True)
    tables = jnp.broadcast_to(
        jnp.stack((background, dispersion))[None], (wave_count, 2, wave_span)
    )
    tables = lax.all_to_all(tables, "wave", 0, 0, tiled=True)
    full_background = tables[:, 0].reshape(length)
    full_dispersion = tables[:, 1].reshape(length)

    spectra = jnp.transpose(pieces, (1, 2, 3, 0, 4)).reshape(2, row_count, sub_pix, length)
    real_part = spectra[0].astype(jnp.float32) - full_background
    imag_part = spectra[1].astype(jnp.float32)
    cosine = jnp.cos(full_dispersion)
    sine_part = jnp.sin(full_dispersion)
    turned_real = real_part * cosine - imag_part * sine_part
    turned_imag = real_part * sine_part + imag_part * cosine

    shape = (row_count, sub_pix, first, second)
    turned_real = turned_real.reshape(shape)
    turned_imag = turned_imag.reshape(shape)
    index_first = jnp.arange(first, dtype=jnp.int32)
    index_second = jnp.arange(second, dtype=jnp.int32)
    small_cos, small_sin = twiddle_table(index_first, index_first, first)
    stage_real, stage_imag = complex_contract(
        "rsak,az->rszk", turned_real, turned_imag, small_cos, small_sin
    )
    turn_cos, turn_sin = twiddle_table(index_first, index_second, length)
    mixed_real = stage_real * turn_cos - stage_imag * turn_sin
    mixed_imag = stage_real * turn_sin + stage_imag * turn_cos
    big_cos, big_sin = twiddle_table(
        index_second, index_second, second, 1.0 / math.sqrt(length)
    )
    out_real, out_imag = complex_contract(
        "rszk,kt->trsz", mixed_real, mixed_imag, big_cos, big_sin
    )
    depth_bf = jnp.stack((out_real, out_imag), axis=1).astype(jnp.bfloat16)
    arrived = lax.all_to_all(depth_bf, ("wave", "pix"), 0, 0, tiled=True)
    arrived = arrived.reshape(wave_count, pix_count, 2, row_count, sub_pix, first)
    depth_field = jnp.transpose(arrived, (2, 3, 5, 1, 0, 4)).reshape(
        2, row_count, first, pix_count * pix_local
    )
    column_piece = lax.all_gather(propagator, "pix", axis=2, tiled=True)
    depth_real = depth_field[0]
    depth_imag = depth_field[1]
    left = jnp.stack(
        (
            jnp.concatenate((depth_real, -depth_imag), axis=-1),
            jnp.concatenate((depth_imag, depth_real), axis=-1),
        )
    )
    stacked = column_piece.reshape(2 * column_piece.shape[1], column_piece.shape[2])
    return jnp.einsum("crzp,pq->crzq", left, stacked, preferred_element_type=jnp.float32)


def solution(mesh):
    in_specs = (P(None, None, "wave", "pix"), P("wave"), P("wave"), P(None, None, "pix"))
    out_specs = P(None, None, ("wave", "pix"), None)
    return jax.shard_map(
        on_device, mesh=mesh, in_specs=in_specs, out_specs=out_specs, check_vma=False
    )
```

```python
import math

import jax
import jax.numpy as jnp
from jax import lax
from jax.sharding import PartitionSpec as P

HIGHEST_PRECISION = lax.Precision.HIGHEST


def twiddle_table(left_index, right_index, modulus, scale=1.0):
    product = left_index[:, None] * right_index[None, :] % modulus
    phase_angle = -2.0 * math.pi / modulus * product.astype(jnp.float32)
    return (jnp.cos(phase_angle) * scale, jnp.sin(phase_angle) * scale)


def complex_contract(spec, real, imag, cosine, sine_part):
    def dot(a, b):
        return jnp.einsum(spec, a, b, precision=HIGHEST_PRECISION)

    return (dot(real, cosine) - dot(imag, sine_part), dot(real, sine_part) + dot(imag, cosine))


def on_device(raw_spectra, background, dispersion, propagator):
    row_count = raw_spectra.shape[1]
    wave_span = raw_spectra.shape[2]
    pix_local = raw_spectra.shape[3]
    wave_count = lax.axis_size("wave")
    pix_count = lax.axis_size("pix")
    devices = wave_count * pix_count
    length = wave_span * wave_count
    sub_pix = pix_local // wave_count
    first = length // devices
    second = devices

    pieces = raw_spectra.reshape(2, row_count, wave_span, wave_count, sub_pix)
    pieces = jnp.transpose(pieces, (3, 0, 1, 4, 2))
    pieces = lax.all_to_all(pieces, "wave", 0, 0, tiled=True)
    tables = jnp.broadcast_to(
        jnp.stack((background, dispersion))[None], (wave_count, 2, wave_span)
    )
    tables = lax.all_to_all(tables, "wave", 0, 0, tiled=True)
    full_background = tables[:, 0].reshape(length)
    full_dispersion = tables[:, 1].reshape(length)

    half_rows = propagator.shape[1] // 2
    permuted_rows, pieces = lax.optimization_barrier((propagator[:, half_rows:], pieces))
    held = gather_held(permuted_rows, wave_count, pix_count)

    spectra = jnp.transpose(pieces, (1, 2, 3, 0, 4)).reshape(2, row_count, sub_pix, length)
    real_part = spectra[0].astype(jnp.float32) - full_background
    imag_part = spectra[1].astype(jnp.float32)
    cosine = jnp.cos(full_dispersion)
    sine_part = jnp.sin(full_dispersion)
    turned_real = real_part * cosine - imag_part * sine_part
    turned_imag = real_part * sine_part + imag_part * cosine

    shape = (row_count, sub_pix, first, second)
    turned_real = turned_real.reshape(shape)
    turned_imag = turned_imag.reshape(shape)
    index_first = jnp.arange(first, dtype=jnp.int32)
    index_second = jnp.arange(second, dtype=jnp.int32)
    small_cos, small_sin = twiddle_table(index_first, index_first, first)
    stage_real, stage_imag = complex_contract(
        "rsak,az->rszk", turned_real, turned_imag, small_cos, small_sin
    )
    turn_cos, turn_sin = twiddle_table(index_first, index_second, length)
    mixed_real = stage_real * turn_cos - stage_imag * turn_sin
    mixed_imag = stage_real * turn_sin + stage_imag * turn_cos
    big_cos, big_sin = twiddle_table(
        index_second, index_second, second, 1.0 / math.sqrt(length)
    )
    out_real, out_imag = complex_contract(
        "rszk,kt->trsz", mixed_real, mixed_imag, big_cos, big_sin
    )
    depth_bf = jnp.stack((out_real, out_imag), axis=1).astype(jnp.bfloat16)
    held, depth_bf = lax.optimization_barrier((held, depth_bf))
    arrived = lax.all_to_all(depth_bf, ("wave", "pix"), 0, 0, tiled=True)
    arrived = arrived.reshape(wave_count, pix_count, 2, row_count, sub_pix, first)
    depth_field = jnp.transpose(arrived, (2, 3, 5, 1, 0, 4)).reshape(
        2, row_count, first, pix_count * pix_local
    )
    upper = lax.all_gather(propagator[:, :half_rows], "pix", axis=2, tiled=True)
    sibling = swap_cores(held, wave_count, pix_count)
    lower = jnp.stack((held, sibling), axis=1)
    chip_count = pix_count // 2
    pix_pos = lax.axis_index("pix")
    order = [(-offset) % chip_count for offset in range(chip_count)]
    lower = lower[jnp.array(order, dtype=jnp.int32)]
    lower = jnp.roll(lower, (pix_pos // 2, pix_pos % 2), axis=(0, 1))
    lower = jnp.transpose(lower, (2, 3, 0, 1, 4)).reshape(upper.shape)
    depth_real = depth_field[0]
    depth_imag = depth_field[1]
    left = jnp.stack(
        (
            jnp.stack((depth_real, -depth_imag), axis=2),
            jnp.stack((depth_imag, depth_real), axis=2),
        )
    )
    image = jnp.einsum(
        "drzcp,cpq->drzq", left[..., :half_rows], upper, preferred_element_type=jnp.float32
    )
    return image + jnp.einsum(
        "drzcp,cpq->drzq", left[..., half_rows:], lower, preferred_element_type=jnp.float32
    )


def flat_index(wave, pix, pix_count):
    return wave * pix_count + pix


def gather_held(piece, wave_count, pix_count):
    chip_count = pix_count // 2
    held = [piece]
    for offset in range(1, chip_count):
        pairs = []
        for wave in range(wave_count):
            for pix in range(pix_count):
                target_chip = (pix // 2 + offset) % chip_count
                target_wave = wave if offset % 2 == 0 else wave ^ 1
                pairs.append(
                    (
                        flat_index(wave, pix, pix_count),
                        flat_index(target_wave, 2 * target_chip + pix % 2, pix_count),
                    )
                )
        held.append(lax.ppermute(piece, ("wave", "pix"), pairs))
    return jnp.stack(held)


def swap_cores(held, wave_count, pix_count):
    pairs = [
        (flat_index(wave, pix, pix_count), flat_index(wave, pix ^ 1, pix_count))
        for wave in range(wave_count)
        for pix in range(pix_count)
    ]
    return lax.ppermute(held, ("wave", "pix"), pairs)


def solution(mesh):
    in_specs = (P(None, None, "wave", "pix"), P("wave"), P("wave"), P(None, None, "pix"))
    out_specs = P(None, None, ("wave", "pix"), None)
    return jax.shard_map(
        on_device, mesh=mesh, in_specs=in_specs, out_specs=out_specs, check_vma=False
    )
```

```python
import math

import jax
import jax.numpy as jnp
from jax import lax
from jax.sharding import PartitionSpec as P

MATMUL_PRECISION = lax.Precision.HIGH


def twiddle_table(left_index, right_index, modulus, scale=1.0):
    product = left_index[:, None] * right_index[None, :] % modulus
    phase_angle = -2.0 * math.pi / modulus * product.astype(jnp.float32)
    return (jnp.cos(phase_angle) * scale, jnp.sin(phase_angle) * scale)


def complex_contract(spec, real, imag, cosine, sine_part):
    def dot(a, b):
        return jnp.einsum(spec, a, b, precision=MATMUL_PRECISION)

    return (dot(real, cosine) - dot(imag, sine_part), dot(real, sine_part) + dot(imag, cosine))


def on_device(raw_spectra, background, dispersion, propagator):
    row_count = raw_spectra.shape[1]
    wave_span = raw_spectra.shape[2]
    pix_local = raw_spectra.shape[3]
    wave_count = lax.axis_size("wave")
    pix_count = lax.axis_size("pix")
    devices = wave_count * pix_count
    length = wave_span * wave_count
    sub_pix = pix_local // wave_count
    first = length // devices
    second = devices

    pieces = raw_spectra.reshape(2, row_count, wave_span, wave_count, sub_pix)
    pieces = jnp.transpose(pieces, (3, 0, 1, 4, 2))
    pieces = lax.all_to_all(pieces, "wave", 0, 0, tiled=True)
    tables = jnp.broadcast_to(
        jnp.stack((background, dispersion))[None], (wave_count, 2, wave_span)
    )
    tables = lax.all_to_all(tables, "wave", 0, 0, tiled=True)
    full_background = tables[:, 0].reshape(length)
    full_dispersion = tables[:, 1].reshape(length)

    spectra = jnp.transpose(pieces, (1, 2, 3, 0, 4)).reshape(2, row_count, sub_pix, length)
    real_part = spectra[0].astype(jnp.float32) - full_background
    imag_part = spectra[1].astype(jnp.float32)
    cosine = jnp.cos(full_dispersion)
    sine_part = jnp.sin(full_dispersion)
    turned_real = real_part * cosine - imag_part * sine_part
    turned_imag = real_part * sine_part + imag_part * cosine

    shape = (row_count, sub_pix, first, second)
    turned_real = turned_real.reshape(shape)
    turned_imag = turned_imag.reshape(shape)
    index_first = jnp.arange(first, dtype=jnp.int32)
    index_second = jnp.arange(second, dtype=jnp.int32)
    small_cos, small_sin = twiddle_table(index_first, index_first, first)
    stage_real, stage_imag = complex_contract(
        "rsak,az->rszk", turned_real, turned_imag, small_cos, small_sin
    )
    turn_cos, turn_sin = twiddle_table(index_first, index_second, length)
    mixed_real = stage_real * turn_cos - stage_imag * turn_sin
    mixed_imag = stage_real * turn_sin + stage_imag * turn_cos
    big_cos, big_sin = twiddle_table(
        index_second, index_second, second, 1.0 / math.sqrt(length)
    )
    out_real, out_imag = complex_contract(
        "rszk,kt->trsz", mixed_real, mixed_imag, big_cos, big_sin
    )
    depth_bf = jnp.stack((out_real, out_imag), axis=1).astype(jnp.bfloat16)
    arrived = lax.all_to_all(depth_bf, ("wave", "pix"), 0, 0, tiled=True)
    arrived = arrived.reshape(wave_count, pix_count, 2, row_count, sub_pix, first)
    depth_field = jnp.transpose(arrived, (2, 3, 5, 1, 0, 4)).reshape(
        2, row_count, first, pix_count * pix_local
    )
    column_piece = lax.all_gather(propagator, "pix", axis=2, tiled=True)
    depth_real = depth_field[0]
    depth_imag = depth_field[1]
    left = jnp.stack(
        (
            jnp.concatenate((depth_real, -depth_imag), axis=-1),
            jnp.concatenate((depth_imag, depth_real), axis=-1),
        )
    )
    stacked = column_piece.reshape(2 * column_piece.shape[1], column_piece.shape[2])
    return jnp.einsum("crzp,pq->crzq", left, stacked, preferred_element_type=jnp.float32)


def solution(mesh):
    in_specs = (P(None, None, "wave", "pix"), P("wave"), P("wave"), P(None, None, "pix"))
    out_specs = P(None, None, ("wave", "pix"), None)
    return jax.shard_map(
        on_device, mesh=mesh, in_specs=in_specs, out_specs=out_specs, check_vma=False
    )
```

```python
import math

import jax
import jax.numpy as jnp
from jax import lax
from jax.experimental import pallas as pl
from jax.experimental.pallas import tpu as pltpu
from jax.sharding import PartitionSpec as P

MATMUL_PRECISION = lax.Precision.HIGH


def twiddle_table(left_index, right_index, modulus, scale=1.0):
    product = left_index[:, None] * right_index[None, :] % modulus
    phase_angle = -2.0 * math.pi / modulus * product.astype(jnp.float32)
    return (jnp.cos(phase_angle) * scale, jnp.sin(phase_angle) * scale)


def complex_contract(spec, real, imag, cosine, sine_part):
    def dot(a, b):
        return jnp.einsum(spec, a, b, precision=MATMUL_PRECISION)

    return (dot(real, cosine) - dot(imag, sine_part), dot(real, sine_part) + dot(imag, cosine))


def on_device(raw_spectra, background, dispersion, propagator):
    row_count = raw_spectra.shape[1]
    wave_span = raw_spectra.shape[2]
    pix_local = raw_spectra.shape[3]
    wave_count = lax.axis_size("wave")
    pix_count = lax.axis_size("pix")
    devices = wave_count * pix_count
    length = wave_span * wave_count
    sub_pix = pix_local // wave_count
    first = length // devices
    second = devices

    pieces = raw_spectra.reshape(2, row_count, wave_span, wave_count, sub_pix)
    pieces = jnp.transpose(pieces, (3, 0, 1, 4, 2))
    pieces = lax.all_to_all(pieces, "wave", 0, 0, tiled=True)
    tables = jnp.broadcast_to(
        jnp.stack((background, dispersion))[None], (wave_count, 2, wave_span)
    )
    tables = lax.all_to_all(tables, "wave", 0, 0, tiled=True)
    full_background = tables[:, 0].reshape(length)
    full_dispersion = tables[:, 1].reshape(length)

    spectra = jnp.transpose(pieces, (1, 2, 3, 0, 4)).reshape(2, row_count, sub_pix, length)
    real_part = spectra[0].astype(jnp.float32) - full_background
    imag_part = spectra[1].astype(jnp.float32)
    cosine = jnp.cos(full_dispersion)
    sine_part = jnp.sin(full_dispersion)
    turned_real = real_part * cosine - imag_part * sine_part
    turned_imag = real_part * sine_part + imag_part * cosine

    shape = (row_count, sub_pix, first, second)
    turned_real = turned_real.reshape(shape)
    turned_imag = turned_imag.reshape(shape)
    index_first = jnp.arange(first, dtype=jnp.int32)
    index_second = jnp.arange(second, dtype=jnp.int32)
    small_cos, small_sin = twiddle_table(index_first, index_first, first)
    stage_real, stage_imag = complex_contract(
        "rsak,az->rszk", turned_real, turned_imag, small_cos, small_sin
    )
    turn_cos, turn_sin = twiddle_table(index_first, index_second, length)
    mixed_real = stage_real * turn_cos - stage_imag * turn_sin
    mixed_imag = stage_real * turn_sin + stage_imag * turn_cos
    big_cos, big_sin = twiddle_table(
        index_second, index_second, second, 1.0 / math.sqrt(length)
    )
    out_real, out_imag = complex_contract(
        "rszk,kt->trsz", mixed_real, mixed_imag, big_cos, big_sin
    )
    depth_bf = jnp.stack((out_real, out_imag), axis=1).astype(jnp.bfloat16)
    arrived = lax.all_to_all(depth_bf, ("wave", "pix"), 0, 0, tiled=True)
    arrived = arrived.reshape(wave_count, pix_count, 2, row_count, sub_pix, first)
    depth_field = jnp.transpose(arrived, (2, 3, 5, 1, 0, 4)).reshape(
        2, row_count, first, pix_count * pix_local
    )
    column_piece = lax.all_gather(propagator, "pix", axis=2, tiled=True)
    depth_real = depth_field[0]
    depth_imag = depth_field[1]
    left = jnp.stack(
        (
            jnp.concatenate((depth_real, -depth_imag), axis=-1),
            jnp.concatenate((depth_imag, depth_real), axis=-1),
        )
    )
    stacked = column_piece.reshape(2 * column_piece.shape[1], column_piece.shape[2])
    image = image_product(left.reshape(-1, stacked.shape[0]), stacked)
    return image.reshape(left.shape[:-1] + (stacked.shape[1],))


def image_kernel(left_ref, right_ref, out_ref):
    out_ref[...] = jnp.dot(left_ref[...], right_ref[...], preferred_element_type=jnp.float32)


def image_product(left, right, tile=256):
    rows, depth = left.shape
    columns = right.shape[1]
    return pl.pallas_call(
        image_kernel,
        out_shape=jax.ShapeDtypeStruct((rows, columns), jnp.float32),
        grid=(columns // tile,),
        in_specs=[
            pl.BlockSpec((rows, depth), lambda j: (0, 0)),
            pl.BlockSpec((depth, tile), lambda j: (0, j)),
        ],
        out_specs=pl.BlockSpec((rows, tile), lambda j: (0, j)),
        cost_estimate=pl.CostEstimate(
            flops=2 * rows * depth * columns,
            transcendentals=0,
            bytes_accessed=2 * rows * depth + 2 * depth * columns + 4 * rows * columns,
        ),
    )(left, right)


def solution(mesh):
    in_specs = (P(None, None, "wave", "pix"), P("wave"), P("wave"), P(None, None, "pix"))
    out_specs = P(None, None, ("wave", "pix"), None)
    return jax.shard_map(
        on_device, mesh=mesh, in_specs=in_specs, out_specs=out_specs, check_vma=False
    )
```

```python
import math

import jax
import jax.numpy as jnp
from jax import lax
from jax.sharding import PartitionSpec as P

HIGHEST_PRECISION = lax.Precision.HIGHEST


def twiddle_table(left_index, right_index, modulus, scale=1.0):
    product = left_index[:, None] * right_index[None, :] % modulus
    phase_angle = -2.0 * math.pi / modulus * product.astype(jnp.float32)
    return (jnp.cos(phase_angle) * scale, jnp.sin(phase_angle) * scale)


def complex_contract(spec, real, imag, cosine, sine_part):
    def dot(a, b):
        return jnp.einsum(spec, a, b, precision=HIGHEST_PRECISION)

    return (dot(real, cosine) - dot(imag, sine_part), dot(real, sine_part) + dot(imag, cosine))


def on_device(raw_spectra, background, dispersion, propagator):
    row_count = raw_spectra.shape[1]
    wave_span = raw_spectra.shape[2]
    pix_local = raw_spectra.shape[3]
    wave_count = lax.axis_size("wave")
    pix_count = lax.axis_size("pix")
    devices = wave_count * pix_count
    length = wave_span * wave_count
    sub_pix = pix_local // wave_count
    first = length // devices
    second = devices

    pieces = raw_spectra.reshape(2, row_count, wave_span, wave_count, sub_pix)
    pieces = jnp.transpose(pieces, (3, 0, 1, 4, 2))
    pieces = lax.all_to_all(pieces, "wave", 0, 0, tiled=True)
    tables = jnp.broadcast_to(
        jnp.stack((background, dispersion))[None], (wave_count, 2, wave_span)
    )
    tables = lax.all_to_all(tables, "wave", 0, 0, tiled=True)
    full_background = tables[:, 0].reshape(length)
    full_dispersion = tables[:, 1].reshape(length)

    spectra = jnp.transpose(pieces, (1, 2, 3, 0, 4)).reshape(2, row_count, sub_pix, length)
    real_part = spectra[0].astype(jnp.float32) - full_background
    imag_part = spectra[1].astype(jnp.float32)
    cosine = jnp.cos(full_dispersion)
    sine_part = jnp.sin(full_dispersion)
    turned_real = real_part * cosine - imag_part * sine_part
    turned_imag = real_part * sine_part + imag_part * cosine

    shape = (row_count, sub_pix, first, second)
    turned_real = turned_real.reshape(shape)
    turned_imag = turned_imag.reshape(shape)
    index_first = jnp.arange(first, dtype=jnp.int32)
    index_second = jnp.arange(second, dtype=jnp.int32)
    small_cos, small_sin = twiddle_table(index_first, index_first, first)
    stage_real, stage_imag = complex_contract(
        "rsak,az->rszk", turned_real, turned_imag, small_cos, small_sin
    )
    turn_cos, turn_sin = twiddle_table(index_first, index_second, length)
    mixed_real = stage_real * turn_cos - stage_imag * turn_sin
    mixed_imag = stage_real * turn_sin + stage_imag * turn_cos
    big_cos, big_sin = twiddle_table(
        index_second, index_second, second, 1.0 / math.sqrt(length)
    )
    out_real, out_imag = complex_contract(
        "rszk,kt->trsz", mixed_real, mixed_imag, big_cos, big_sin
    )
    depth_bf = jnp.stack((out_real, out_imag), axis=1).astype(jnp.bfloat16)
    arrived = lax.all_to_all(depth_bf, ("wave", "pix"), 0, 0, tiled=True)
    shared_rows = propagator.shape[1] // 4
    gathered_rows = propagator.shape[1] - shared_rows
    permuted_rows, arrived = lax.optimization_barrier((propagator[:, gathered_rows:], arrived))
    held = gather_held(permuted_rows, wave_count, pix_count)
    sibling = swap_cores(held, wave_count, pix_count)
    arrived = arrived.reshape(wave_count, pix_count, 2, row_count, sub_pix, first)
    depth_field = jnp.transpose(arrived, (2, 3, 5, 1, 0, 4)).reshape(
        2, row_count, first, pix_count * pix_local
    )
    upper = lax.all_gather(propagator[:, :gathered_rows], "pix", axis=2, tiled=True)
    depth_real = depth_field[0]
    depth_imag = depth_field[1]
    left = jnp.stack(
        (
            jnp.stack((depth_real, -depth_imag), axis=2),
            jnp.stack((depth_imag, depth_real), axis=2),
        )
    )
    lower_columns = jnp.stack((held, sibling), axis=1)
    lower = jnp.einsum(
        "drzcp,okcpj->drzokj",
        left[..., gathered_rows:],
        lower_columns,
        preferred_element_type=jnp.float32,
    )
    chip_count = pix_count // 2
    pix_pos = lax.axis_index("pix")
    order = [(-offset) % chip_count for offset in range(chip_count)]
    lower = lower[:, :, :, jnp.array(order, dtype=jnp.int32)]
    lower = jnp.roll(lower, (pix_pos // 2, pix_pos % 2), axis=(3, 4))
    lower = lower.reshape(lower.shape[:3] + (pix_count * pix_local,))
    upper = jnp.einsum(
        "drzcp,cpq->drzq", left[..., :gathered_rows], upper, preferred_element_type=jnp.float32
    )
    return upper + lower


def flat_index(wave, pix, pix_count):
    return wave * pix_count + pix


def gather_held(piece, wave_count, pix_count):
    chip_count = pix_count // 2
    held = [piece]
    for offset in range(1, chip_count):
        pairs = []
        for wave in range(wave_count):
            for pix in range(pix_count):
                target_chip = (pix // 2 + offset) % chip_count
                target_wave = wave if offset % 2 == 0 else wave ^ 1
                pairs.append(
                    (
                        flat_index(wave, pix, pix_count),
                        flat_index(target_wave, 2 * target_chip + pix % 2, pix_count),
                    )
                )
        held.append(lax.ppermute(piece, ("wave", "pix"), pairs))
    return jnp.stack(held)


def swap_cores(held, wave_count, pix_count):
    pairs = [
        (flat_index(wave, pix, pix_count), flat_index(wave, pix ^ 1, pix_count))
        for wave in range(wave_count)
        for pix in range(pix_count)
    ]
    return lax.ppermute(held, ("wave", "pix"), pairs)


def solution(mesh):
    in_specs = (P(None, None, "wave", "pix"), P("wave"), P("wave"), P(None, None, "pix"))
    out_specs = P(None, None, ("wave", "pix"), None)
    return jax.shard_map(
        on_device, mesh=mesh, in_specs=in_specs, out_specs=out_specs, check_vma=False
    )
```

```python
import math

import jax
import jax.numpy as jnp
from jax import lax
from jax.sharding import PartitionSpec as P

HIGHEST_PRECISION = lax.Precision.HIGHEST
PIX = ("chip", "core")
ALL = ("wave",) + PIX


def twiddle_table(left_index, right_index, modulus, scale=1.0):
    product = left_index[:, None] * right_index[None, :] % modulus
    phase_angle = -2.0 * math.pi / modulus * product.astype(jnp.float32)
    return (jnp.cos(phase_angle) * scale, jnp.sin(phase_angle) * scale)


def complex_contract(spec, real, imag, cosine, sine_part):
    def dot(a, b):
        return jnp.einsum(spec, a, b, precision=HIGHEST_PRECISION)

    return (dot(real, cosine) - dot(imag, sine_part), dot(real, sine_part) + dot(imag, cosine))


def on_device(raw_spectra, background, dispersion, propagator):
    row_count = raw_spectra.shape[1]
    wave_span = raw_spectra.shape[2]
    pix_local = raw_spectra.shape[3]
    wave_count = lax.axis_size("wave")
    pix_count = lax.axis_size(PIX)
    devices = wave_count * pix_count
    length = wave_span * wave_count
    sub_pix = pix_local // wave_count
    first = length // devices
    second = devices

    pieces = raw_spectra.reshape(2, row_count, wave_span, wave_count, sub_pix)
    pieces = jnp.transpose(pieces, (3, 0, 1, 4, 2))
    pieces = lax.all_to_all(pieces, "wave", 0, 0, tiled=True)
    tables = jnp.broadcast_to(
        jnp.stack((background, dispersion))[None], (wave_count, 2, wave_span)
    )
    tables = lax.all_to_all(tables, "wave", 0, 0, tiled=True)
    full_background = tables[:, 0].reshape(length)
    full_dispersion = tables[:, 1].reshape(length)

    spectra = jnp.transpose(pieces, (1, 2, 3, 0, 4)).reshape(2, row_count, sub_pix, length)
    real_part = spectra[0].astype(jnp.float32) - full_background
    imag_part = spectra[1].astype(jnp.float32)
    cosine = jnp.cos(full_dispersion)
    sine_part = jnp.sin(full_dispersion)
    turned_real = real_part * cosine - imag_part * sine_part
    turned_imag = real_part * sine_part + imag_part * cosine

    shape = (row_count, sub_pix, first, second)
    turned_real = turned_real.reshape(shape)
    turned_imag = turned_imag.reshape(shape)
    index_first = jnp.arange(first, dtype=jnp.int32)
    index_second = jnp.arange(second, dtype=jnp.int32)
    small_cos, small_sin = twiddle_table(index_first, index_first, first)
    stage_real, stage_imag = complex_contract(
        "rsak,az->rszk", turned_real, turned_imag, small_cos, small_sin
    )
    turn_cos, turn_sin = twiddle_table(index_first, index_second, length)
    mixed_real = stage_real * turn_cos - stage_imag * turn_sin
    mixed_imag = stage_real * turn_sin + stage_imag * turn_cos
    big_cos, big_sin = twiddle_table(
        index_second, index_second, second, 1.0 / math.sqrt(length)
    )
    out_real, out_imag = complex_contract(
        "rszk,kt->trsz", mixed_real, mixed_imag, big_cos, big_sin
    )
    depth_bf = jnp.stack((out_real, out_imag), axis=1).astype(jnp.bfloat16)
    arrived = lax.all_to_all(depth_bf, ALL, 0, 0, tiled=True)
    arrived = arrived.reshape(wave_count, pix_count, 2, row_count, sub_pix, first)
    depth_field = jnp.transpose(arrived, (2, 3, 5, 1, 0, 4)).reshape(
        2, row_count, first, pix_count * pix_local
    )
    same_core = lax.all_gather(propagator, "chip", axis=0)
    pairs = [(index, index ^ 1) for index in range(wave_count * pix_count)]
    sibling_depth = lax.ppermute(depth_field, ALL, pairs)
    blocks = jnp.stack((depth_field, sibling_depth), axis=2)
    left = jnp.stack(
        (
            jnp.stack((blocks[0], -blocks[1]), axis=-2),
            jnp.stack((blocks[1], blocks[0]), axis=-2),
        )
    )
    product = jnp.einsum(
        "drbzcp,kcpj->drbzkj", left, same_core, preferred_element_type=jnp.float32
    )
    received = lax.ppermute(product[:, :, 1], ALL, pairs)
    mine = product[:, :, 0]
    own_first = lax.axis_index("core") == 0
    image = jnp.where(
        own_first, jnp.stack((mine, received), axis=4), jnp.stack((received, mine), axis=4)
    )
    return image.reshape(2, row_count, first, pix_count * pix_local)


def solution(mesh):
    wave_count, pix_count = mesh.devices.shape
    split_mesh = jax.sharding.Mesh(mesh.devices.reshape(wave_count, pix_count // 2, 2), ALL)
    in_specs = (P(None, None, "wave", PIX), P("wave"), P("wave"), P(None, None, PIX))
    out_specs = P(None, None, ALL, None)
    return jax.shard_map(
        on_device, mesh=split_mesh, in_specs=in_specs, out_specs=out_specs, check_vma=False
    )
```

```python
import math

import jax
import jax.numpy as jnp
from jax import lax
from jax.sharding import PartitionSpec as P

HIGHEST_PRECISION = lax.Precision.HIGHEST
PIX = ("chip", "core")
ALL = ("wave",) + PIX


def twiddle_table(left_index, right_index, modulus, scale=1.0):
    product = left_index[:, None] * right_index[None, :] % modulus
    phase_angle = -2.0 * math.pi / modulus * product.astype(jnp.float32)
    return (jnp.cos(phase_angle) * scale, jnp.sin(phase_angle) * scale)


def complex_contract(spec, real, imag, cosine, sine_part):
    def dot(a, b):
        return jnp.einsum(spec, a, b, precision=HIGHEST_PRECISION)

    return (dot(real, cosine) - dot(imag, sine_part), dot(real, sine_part) + dot(imag, cosine))


def on_device(raw_spectra, background, dispersion, propagator):
    row_count = raw_spectra.shape[1]
    wave_span = raw_spectra.shape[2]
    pix_local = raw_spectra.shape[3]
    wave_count = lax.axis_size("wave")
    pix_count = lax.axis_size(PIX)
    devices = wave_count * pix_count
    length = wave_span * wave_count
    sub_pix = pix_local // wave_count
    first = length // devices
    second = devices

    pieces = raw_spectra.reshape(2, row_count, wave_span, wave_count, sub_pix)
    pieces = jnp.transpose(pieces, (3, 0, 1, 4, 2))
    pieces = lax.all_to_all(pieces, "wave", 0, 0, tiled=True)
    tables = jnp.broadcast_to(
        jnp.stack((background, dispersion))[None], (wave_count, 2, wave_span)
    )
    tables = lax.all_to_all(tables, "wave", 0, 0, tiled=True)
    full_background = tables[:, 0].reshape(length)
    full_dispersion = tables[:, 1].reshape(length)

    spectra = jnp.transpose(pieces, (1, 2, 3, 0, 4)).reshape(2, row_count, sub_pix, length)
    real_part = spectra[0].astype(jnp.float32) - full_background
    imag_part = spectra[1].astype(jnp.float32)
    cosine = jnp.cos(full_dispersion)
    sine_part = jnp.sin(full_dispersion)
    turned_real = real_part * cosine - imag_part * sine_part
    turned_imag = real_part * sine_part + imag_part * cosine

    shape = (row_count, sub_pix, first, second)
    turned_real = turned_real.reshape(shape)
    turned_imag = turned_imag.reshape(shape)
    index_first = jnp.arange(first, dtype=jnp.int32)
    index_second = jnp.arange(second, dtype=jnp.int32)
    small_cos, small_sin = twiddle_table(index_first, index_first, first)
    stage_real, stage_imag = complex_contract(
        "rsak,az->rszk", turned_real, turned_imag, small_cos, small_sin
    )
    turn_cos, turn_sin = twiddle_table(index_first, index_second, length)
    mixed_real = stage_real * turn_cos - stage_imag * turn_sin
    mixed_imag = stage_real * turn_sin + stage_imag * turn_cos
    big_cos, big_sin = twiddle_table(
        index_second, index_second, second, 1.0 / math.sqrt(length)
    )
    out_real, out_imag = complex_contract(
        "rszk,kt->trsz", mixed_real, mixed_imag, big_cos, big_sin
    )
    depth_bf = jnp.stack((out_real, out_imag), axis=1).astype(jnp.bfloat16)
    arrived = lax.all_to_all(depth_bf, ALL, 0, 0, tiled=True)
    arrived = arrived.reshape(wave_count, pix_count, 2, row_count, sub_pix, first)
    depth_field = jnp.transpose(arrived, (2, 3, 5, 1, 0, 4)).reshape(
        2, row_count, first, pix_count * pix_local
    )
    same_core = lax.all_gather(propagator, "chip", axis=2, tiled=True)
    pairs = [(index, index ^ 1) for index in range(wave_count * pix_count)]
    sibling_depth = lax.ppermute(depth_field, ALL, pairs)
    blocks = jnp.stack((depth_field, sibling_depth), axis=2)
    left = jnp.stack(
        (
            jnp.stack((blocks[0], -blocks[1]), axis=-2),
            jnp.stack((blocks[1], blocks[0]), axis=-2),
        )
    )
    product = jnp.einsum(
        "drbzcp,cpq->drbzq", left, same_core, preferred_element_type=jnp.float32
    )
    chip_count = pix_count // 2
    received = lax.ppermute(product[:, :, 1], ALL, pairs)
    received = received.reshape(received.shape[:-1] + (chip_count, pix_local))
    mine = product[:, :, 0].reshape(received.shape)
    own_first = lax.axis_index("core") == 0
    image = jnp.where(
        own_first, jnp.stack((mine, received), axis=4), jnp.stack((received, mine), axis=4)
    )
    return image.reshape(2, row_count, first, pix_count * pix_local)


def solution(mesh):
    wave_count, pix_count = mesh.devices.shape
    split_mesh = jax.sharding.Mesh(mesh.devices.reshape(wave_count, pix_count // 2, 2), ALL)
    in_specs = (P(None, None, "wave", PIX), P("wave"), P("wave"), P(None, None, PIX))
    out_specs = P(None, None, ALL, None)
    return jax.shard_map(
        on_device, mesh=split_mesh, in_specs=in_specs, out_specs=out_specs, check_vma=False
    )
```

```python
import math

import jax
import jax.numpy as jnp
from jax import lax
from jax.sharding import PartitionSpec as P

HIGHEST_PRECISION = lax.Precision.HIGHEST
PIX = ("chip", "core")
ALL = ("wave",) + PIX


def twiddle_table(left_index, right_index, modulus, scale=1.0):
    product = left_index[:, None] * right_index[None, :] % modulus
    phase_angle = -2.0 * math.pi / modulus * product.astype(jnp.float32)
    return (jnp.cos(phase_angle) * scale, jnp.sin(phase_angle) * scale)


def complex_contract(spec, real, imag, cosine, sine_part):
    def dot(a, b):
        return jnp.einsum(spec, a, b, precision=HIGHEST_PRECISION)

    return (dot(real, cosine) - dot(imag, sine_part), dot(real, sine_part) + dot(imag, cosine))


def on_device(raw_spectra, background, dispersion, propagator):
    row_count = raw_spectra.shape[1]
    wave_span = raw_spectra.shape[2]
    pix_local = raw_spectra.shape[3]
    wave_count = lax.axis_size("wave")
    pix_count = lax.axis_size(PIX)
    devices = wave_count * pix_count
    length = wave_span * wave_count
    sub_pix = pix_local // wave_count
    first = length // devices
    second = devices

    pieces = raw_spectra.reshape(2, row_count, wave_span, wave_count, sub_pix)
    pieces = jnp.transpose(pieces, (3, 0, 1, 4, 2))
    pieces = lax.all_to_all(pieces, "wave", 0, 0, tiled=True)
    tables = jnp.broadcast_to(
        jnp.stack((background, dispersion))[None], (wave_count, 2, wave_span)
    )
    tables = lax.all_to_all(tables, "wave", 0, 0, tiled=True)
    full_background = tables[:, 0].reshape(length)
    full_dispersion = tables[:, 1].reshape(length)

    spectra = jnp.transpose(pieces, (1, 2, 3, 0, 4)).reshape(2, row_count, sub_pix, length)
    real_part = spectra[0].astype(jnp.float32) - full_background
    imag_part = spectra[1].astype(jnp.float32)
    cosine = jnp.cos(full_dispersion)
    sine_part = jnp.sin(full_dispersion)
    turned_real = real_part * cosine - imag_part * sine_part
    turned_imag = real_part * sine_part + imag_part * cosine

    shape = (row_count, sub_pix, first, second)
    turned_real = turned_real.reshape(shape)
    turned_imag = turned_imag.reshape(shape)
    index_first = jnp.arange(first, dtype=jnp.int32)
    index_second = jnp.arange(second, dtype=jnp.int32)
    small_cos, small_sin = twiddle_table(index_first, index_first, first)
    stage_real, stage_imag = complex_contract(
        "rsak,az->rszk", turned_real, turned_imag, small_cos, small_sin
    )
    turn_cos, turn_sin = twiddle_table(index_first, index_second, length)
    mixed_real = stage_real * turn_cos - stage_imag * turn_sin
    mixed_imag = stage_real * turn_sin + stage_imag * turn_cos
    big_cos, big_sin = twiddle_table(
        index_second, index_second, second, 1.0 / math.sqrt(length)
    )
    out_real, out_imag = complex_contract(
        "rszk,kt->trsz", mixed_real, mixed_imag, big_cos, big_sin
    )
    depth_bf = jnp.stack((out_real, out_imag), axis=1).astype(jnp.bfloat16)
    arrived = lax.all_to_all(depth_bf, ALL, 0, 0, tiled=True)
    arrived = arrived.reshape(wave_count, pix_count, 2, row_count, sub_pix, first)
    depth_field = jnp.transpose(arrived, (2, 3, 5, 1, 0, 4)).reshape(
        2, row_count, first, pix_count * pix_local
    )
    same_core = lax.all_gather(jnp.transpose(propagator, (2, 0, 1)), "chip", axis=0)
    same_core = same_core.reshape(-1, 2, propagator.shape[1])
    pairs = [(index, index ^ 1) for index in range(wave_count * pix_count)]
    sibling_depth = lax.ppermute(depth_field, ALL, pairs)
    blocks = jnp.stack((depth_field, sibling_depth), axis=2)
    left = jnp.stack(
        (
            jnp.stack((blocks[0], -blocks[1]), axis=-2),
            jnp.stack((blocks[1], blocks[0]), axis=-2),
        )
    )
    chip_count = pix_count // 2

    def product(block):
        result = jnp.einsum(
            "drzcp,qcp->drzq", left[:, :, block], same_core, preferred_element_type=jnp.float32
        )
        return result.reshape(result.shape[:-1] + (chip_count, pix_local))

    received = lax.ppermute(product(1), ALL, pairs)
    mine = product(0)
    own_first = lax.axis_index("core") == 0
    image = jnp.where(
        own_first, jnp.stack((mine, received), axis=4), jnp.stack((received, mine), axis=4)
    )
    return image.reshape(2, row_count, first, pix_count * pix_local)


def solution(mesh):
    wave_count, pix_count = mesh.devices.shape
    split_mesh = jax.sharding.Mesh(mesh.devices.reshape(wave_count, pix_count // 2, 2), ALL)
    in_specs = (P(None, None, "wave", PIX), P("wave"), P("wave"), P(None, None, PIX))
    out_specs = P(None, None, ALL, None)
    return jax.shard_map(
        on_device, mesh=split_mesh, in_specs=in_specs, out_specs=out_specs, check_vma=False
    )
```

```python
import math

import jax
import jax.numpy as jnp
from jax import lax
from jax.sharding import PartitionSpec as P

HIGHEST_PRECISION = lax.Precision.HIGHEST
PIX = ("chip", "core")
ALL = ("wave",) + PIX


def twiddle_table(left_index, right_index, modulus, scale=1.0):
    product = left_index[:, None] * right_index[None, :] % modulus
    phase_angle = -2.0 * math.pi / modulus * product.astype(jnp.float32)
    return (jnp.cos(phase_angle) * scale, jnp.sin(phase_angle) * scale)


def complex_contract(spec, real, imag, cosine, sine_part):
    def dot(a, b):
        return jnp.einsum(spec, a, b, precision=HIGHEST_PRECISION)

    return (dot(real, cosine) - dot(imag, sine_part), dot(real, sine_part) + dot(imag, cosine))


def on_device(raw_spectra, background, dispersion, propagator):
    row_count = raw_spectra.shape[1]
    wave_span = raw_spectra.shape[2]
    pix_local = raw_spectra.shape[3]
    wave_count = lax.axis_size("wave")
    pix_count = lax.axis_size(PIX)
    devices = wave_count * pix_count
    length = wave_span * wave_count
    sub_pix = pix_local // wave_count
    first = length // devices
    second = devices

    pieces = raw_spectra.reshape(2, row_count, wave_span, wave_count, sub_pix)
    pieces = jnp.transpose(pieces, (3, 0, 1, 4, 2))
    pieces = lax.all_to_all(pieces, "wave", 0, 0, tiled=True)
    tables = jnp.broadcast_to(
        jnp.stack((background, dispersion))[None], (wave_count, 2, wave_span)
    )
    tables = lax.all_to_all(tables, "wave", 0, 0, tiled=True)
    full_background = tables[:, 0].reshape(length)
    full_dispersion = tables[:, 1].reshape(length)

    spectra = jnp.transpose(pieces, (1, 2, 3, 0, 4)).reshape(2, row_count, sub_pix, length)
    real_part = spectra[0].astype(jnp.float32) - full_background
    imag_part = spectra[1].astype(jnp.float32)
    cosine = jnp.cos(full_dispersion)
    sine_part = jnp.sin(full_dispersion)
    turned_real = real_part * cosine - imag_part * sine_part
    turned_imag = real_part * sine_part + imag_part * cosine

    shape = (row_count, sub_pix, first, second)
    turned_real = turned_real.reshape(shape)
    turned_imag = turned_imag.reshape(shape)
    index_first = jnp.arange(first, dtype=jnp.int32)
    index_second = jnp.arange(second, dtype=jnp.int32)
    small_cos, small_sin = twiddle_table(index_first, index_first, first)
    stage_real, stage_imag = complex_contract(
        "rsak,az->rszk", turned_real, turned_imag, small_cos, small_sin
    )
    turn_cos, turn_sin = twiddle_table(index_first, index_second, length)
    mixed_real = stage_real * turn_cos - stage_imag * turn_sin
    mixed_imag = stage_real * turn_sin + stage_imag * turn_cos
    big_cos, big_sin = twiddle_table(
        index_second, index_second, second, 1.0 / math.sqrt(length)
    )
    out_real, out_imag = complex_contract(
        "rszk,kt->trsz", mixed_real, mixed_imag, big_cos, big_sin
    )
    depth_bf = jnp.stack((out_real, out_imag), axis=1).astype(jnp.bfloat16)
    arrived = lax.all_to_all(depth_bf, ALL, 0, 0, tiled=True)
    arrived = arrived.reshape(wave_count, pix_count, 2, row_count, sub_pix, first)
    depth_field = jnp.transpose(arrived, (2, 3, 5, 1, 0, 4)).reshape(
        2, row_count, first, pix_count * pix_local
    )
    same_core = lax.all_gather(jnp.transpose(propagator, (2, 0, 1)), "chip", axis=0)
    same_core = same_core.reshape(-1, 2, propagator.shape[1])
    pairs = [(index, index ^ 1) for index in range(wave_count * pix_count)]
    sibling_depth = lax.ppermute(depth_field, ALL, pairs)
    blocks = jnp.stack((depth_field, sibling_depth), axis=2)
    left = jnp.stack(
        (
            jnp.stack((blocks[0], -blocks[1]), axis=-2),
            jnp.stack((blocks[1], blocks[0]), axis=-2),
        )
    )
    chip_count = pix_count // 2

    def product(block):
        result = jnp.einsum(
            "drzcp,qcp->drzq", left[:, :, block], same_core, preferred_element_type=jnp.float32
        )
        return result.reshape(result.shape[:-1] + (chip_count, pix_local))

    received = lax.ppermute(product(1), ALL, pairs)
    mine = product(0)
    wide_shape = mine.shape[:-1] + (2, pix_local)
    width = pix_count * pix_local
    mine = jnp.broadcast_to(mine[..., None, :], wide_shape).reshape(2, row_count, first, width)
    received = jnp.broadcast_to(received[..., None, :], wide_shape).reshape(mine.shape)
    block_core = jnp.arange(width, dtype=jnp.int32) // pix_local % 2
    return jnp.where(block_core == lax.axis_index("core"), mine, received)


def solution(mesh):
    wave_count, pix_count = mesh.devices.shape
    split_mesh = jax.sharding.Mesh(mesh.devices.reshape(wave_count, pix_count // 2, 2), ALL)
    in_specs = (P(None, None, "wave", PIX), P("wave"), P("wave"), P(None, None, PIX))
    out_specs = P(None, None, ALL, None)
    return jax.shard_map(
        on_device, mesh=split_mesh, in_specs=in_specs, out_specs=out_specs, check_vma=False
    )
```

```python
import math

import jax
import jax.numpy as jnp
from jax import lax
from jax.sharding import PartitionSpec as P

HIGHEST_PRECISION = lax.Precision.HIGHEST
PIX = ("chip", "core")
ALL = ("wave",) + PIX


def twiddle_table(left_index, right_index, modulus, scale=1.0):
    product = left_index[:, None] * right_index[None, :] % modulus
    phase_angle = -2.0 * math.pi / modulus * product.astype(jnp.float32)
    return (jnp.cos(phase_angle) * scale, jnp.sin(phase_angle) * scale)


def complex_contract(spec, real, imag, cosine, sine_part):
    def dot(a, b):
        return jnp.einsum(spec, a, b, precision=HIGHEST_PRECISION)

    return (dot(real, cosine) - dot(imag, sine_part), dot(real, sine_part) + dot(imag, cosine))


def on_device(raw_spectra, background, dispersion, propagator):
    row_count = raw_spectra.shape[1]
    wave_span = raw_spectra.shape[2]
    pix_local = raw_spectra.shape[3]
    wave_count = lax.axis_size("wave")
    pix_count = lax.axis_size(PIX)
    devices = wave_count * pix_count
    length = wave_span * wave_count
    sub_pix = pix_local // wave_count
    first = length // devices
    second = devices

    pieces = raw_spectra.reshape(2, row_count, wave_span, wave_count, sub_pix)
    pieces = jnp.transpose(pieces, (3, 0, 1, 4, 2))
    pieces = lax.all_to_all(pieces, "wave", 0, 0, tiled=True)
    tables = jnp.broadcast_to(
        jnp.stack((background, dispersion))[None], (wave_count, 2, wave_span)
    )
    tables = lax.all_to_all(tables, "wave", 0, 0, tiled=True)
    full_background = tables[:, 0].reshape(length)
    full_dispersion = tables[:, 1].reshape(length)

    spectra = jnp.transpose(pieces, (1, 2, 3, 0, 4)).reshape(2, row_count, sub_pix, length)
    real_part = spectra[0].astype(jnp.float32) - full_background
    imag_part = spectra[1].astype(jnp.float32)
    cosine = jnp.cos(full_dispersion)
    sine_part = jnp.sin(full_dispersion)
    turned_real = real_part * cosine - imag_part * sine_part
    turned_imag = real_part * sine_part + imag_part * cosine

    shape = (row_count, sub_pix, first, second)
    turned_real = turned_real.reshape(shape)
    turned_imag = turned_imag.reshape(shape)
    index_first = jnp.arange(first, dtype=jnp.int32)
    index_second = jnp.arange(second, dtype=jnp.int32)
    small_cos, small_sin = twiddle_table(index_first, index_first, first)
    stage_real, stage_imag = complex_contract(
        "rsak,az->rszk", turned_real, turned_imag, small_cos, small_sin
    )
    turn_cos, turn_sin = twiddle_table(index_first, index_second, length)
    mixed_real = stage_real * turn_cos - stage_imag * turn_sin
    mixed_imag = stage_real * turn_sin + stage_imag * turn_cos
    big_cos, big_sin = twiddle_table(
        index_second, index_second, second, 1.0 / math.sqrt(length)
    )
    out_real, out_imag = complex_contract(
        "rszk,kt->trsz", mixed_real, mixed_imag, big_cos, big_sin
    )
    depth_bf = jnp.stack((out_real, out_imag), axis=1).astype(jnp.bfloat16)
    arrived = lax.all_to_all(depth_bf, ALL, 0, 0, tiled=True)
    arrived = arrived.reshape(wave_count, pix_count, 2, row_count, sub_pix, first)
    depth_field = jnp.transpose(arrived, (2, 3, 5, 1, 0, 4)).reshape(
        2, row_count, first, pix_count * pix_local
    )
    same_core = lax.all_gather(propagator, "chip", axis=0)
    pairs = [(index, index ^ 1) for index in range(wave_count * pix_count)]
    sibling_depth = lax.ppermute(depth_field, ALL, pairs)
    blocks = jnp.stack((depth_field, sibling_depth), axis=2)
    left = jnp.stack(
        (
            jnp.stack((blocks[0], -blocks[1]), axis=-2),
            jnp.stack((blocks[1], blocks[0]), axis=-2),
        )
    )
    def product(block):
        return jnp.einsum(
            "drzcp,kcpj->drzkj", left[:, :, block], same_core, preferred_element_type=jnp.float32
        )

    received = lax.ppermute(product(1), ALL, pairs)
    mine = product(0)
    own_first = lax.axis_index("core") == 0
    image = jnp.where(
        own_first, jnp.stack((mine, received), axis=4), jnp.stack((received, mine), axis=4)
    )
    return image.reshape(2, row_count, first, pix_count * pix_local)


def solution(mesh):
    wave_count, pix_count = mesh.devices.shape
    split_mesh = jax.sharding.Mesh(mesh.devices.reshape(wave_count, pix_count // 2, 2), ALL)
    in_specs = (P(None, None, "wave", PIX), P("wave"), P("wave"), P(None, None, PIX))
    out_specs = P(None, None, ALL, None)
    return jax.shard_map(
        on_device, mesh=split_mesh, in_specs=in_specs, out_specs=out_specs, check_vma=False
    )
```

```python
import math

import jax
import jax.numpy as jnp
from jax import lax
from jax.sharding import PartitionSpec as P

MATMUL_PRECISION = lax.Precision.HIGH
PIX = ("chip", "core")
ALL = ("wave",) + PIX


def twiddle_table(left_index, right_index, modulus, scale=1.0):
    product = left_index[:, None] * right_index[None, :] % modulus
    phase_angle = -2.0 * math.pi / modulus * product.astype(jnp.float32)
    return (jnp.cos(phase_angle) * scale, jnp.sin(phase_angle) * scale)


def complex_contract(spec, real, imag, cosine, sine_part):
    def dot(a, b):
        return jnp.einsum(spec, a, b, precision=MATMUL_PRECISION)

    return (dot(real, cosine) - dot(imag, sine_part), dot(real, sine_part) + dot(imag, cosine))


def on_device(raw_spectra, background, dispersion, propagator):
    row_count = raw_spectra.shape[1]
    wave_span = raw_spectra.shape[2]
    pix_local = raw_spectra.shape[3]
    wave_count = lax.axis_size("wave")
    pix_count = lax.axis_size(PIX)
    devices = wave_count * pix_count
    length = wave_span * wave_count
    sub_pix = pix_local // wave_count
    first = length // devices
    second = devices

    pieces = raw_spectra.reshape(2, row_count, wave_span, wave_count, sub_pix)
    pieces = jnp.transpose(pieces, (3, 0, 1, 4, 2))
    pieces = lax.all_to_all(pieces, "wave", 0, 0, tiled=True)
    tables = jnp.broadcast_to(
        jnp.stack((background, dispersion))[None], (wave_count, 2, wave_span)
    )
    tables = lax.all_to_all(tables, "wave", 0, 0, tiled=True)
    full_background = tables[:, 0].reshape(length)
    full_dispersion = tables[:, 1].reshape(length)

    spectra = jnp.transpose(pieces, (1, 2, 3, 0, 4)).reshape(2, row_count, sub_pix, length)
    real_part = spectra[0].astype(jnp.float32) - full_background
    imag_part = spectra[1].astype(jnp.float32)
    cosine = jnp.cos(full_dispersion)
    sine_part = jnp.sin(full_dispersion)
    turned_real = real_part * cosine - imag_part * sine_part
    turned_imag = real_part * sine_part + imag_part * cosine

    shape = (row_count, sub_pix, first, second)
    turned_real = turned_real.reshape(shape)
    turned_imag = turned_imag.reshape(shape)
    index_first = jnp.arange(first, dtype=jnp.int32)
    index_second = jnp.arange(second, dtype=jnp.int32)
    small_cos, small_sin = twiddle_table(index_first, index_first, first)
    stage_real, stage_imag = complex_contract(
        "rsak,az->rszk", turned_real, turned_imag, small_cos, small_sin
    )
    turn_cos, turn_sin = twiddle_table(index_first, index_second, length)
    mixed_real = stage_real * turn_cos - stage_imag * turn_sin
    mixed_imag = stage_real * turn_sin + stage_imag * turn_cos
    big_cos, big_sin = twiddle_table(
        index_second, index_second, second, 1.0 / math.sqrt(length)
    )
    out_real, out_imag = complex_contract(
        "rszk,kt->trsz", mixed_real, mixed_imag, big_cos, big_sin
    )
    depth_bf = jnp.stack((out_real, out_imag), axis=1).astype(jnp.bfloat16)
    arrived = lax.all_to_all(depth_bf, ALL, 0, 0, tiled=True)
    arrived = arrived.reshape(wave_count, pix_count, 2, row_count, sub_pix, first)
    depth_field = jnp.transpose(arrived, (2, 3, 5, 1, 0, 4)).reshape(
        2, row_count, first, pix_count * pix_local
    )
    same_core = lax.all_gather(propagator, "chip", axis=0)
    pairs = [(index, index ^ 1) for index in range(wave_count * pix_count)]
    sibling_depth = lax.ppermute(depth_field, ALL, pairs)
    blocks = jnp.stack((depth_field, sibling_depth), axis=2)
    left = jnp.stack(
        (
            jnp.stack((blocks[0], -blocks[1]), axis=-2),
            jnp.stack((blocks[1], blocks[0]), axis=-2),
        )
    )
    def product(block):
        return jnp.einsum(
            "drzcp,kcpj->drzkj", left[:, :, block], same_core, preferred_element_type=jnp.float32
        )

    received = lax.ppermute(product(1), ALL, pairs)
    mine = product(0)
    own_first = lax.axis_index("core") == 0
    image = jnp.where(
        own_first, jnp.stack((mine, received), axis=4), jnp.stack((received, mine), axis=4)
    )
    return image.reshape(2, row_count, first, pix_count * pix_local)


def solution(mesh):
    wave_count, pix_count = mesh.devices.shape
    split_mesh = jax.sharding.Mesh(mesh.devices.reshape(wave_count, pix_count // 2, 2), ALL)
    in_specs = (P(None, None, "wave", PIX), P("wave"), P("wave"), P(None, None, PIX))
    out_specs = P(None, None, ALL, None)
    return jax.shard_map(
        on_device, mesh=split_mesh, in_specs=in_specs, out_specs=out_specs, check_vma=False
    )
```
